32 devices in a mesh: xy: 16 (over z, y, core), gz: 2 (over x).
Axes of the slice: x: 2, y: 2, z: 4, core: 2. Of those that a mesh axis runs over, the one named last changes fastest.
Arguments:
- hidden_features: bfloat16 [16, 16, 16, 512], P('gz', None, 'xy'), may hold values from -6 to 6
- scaling_factors_prenormal: float32 [512], replicated, may hold values from 0.1 to 1.9
- attention_input_matrices: bfloat16 [3, 512, 1536], P(None, 'xy'), may hold values from -1 to 1
- final_projection_matrices: bfloat16 [3, 512, 512], P(None, 'xy'), may hold values from -0.25 to 0.25
- score_scaling: float32 [3, 8], replicated, may hold values from 0 to 40
- filled_pillar_positions: int32 [16, 16], P('xy'), may hold values from 0 to 15, as said below
- filled_pillar_totals: int32 [16], P('xy'), may hold values from 4 to 16, as said below
Outputs:
- block_out: bfloat16 [16, 16, 16, 512], P('gz', None, 'xy')
The draws below stay inside these ranges and needn't reach their ends.
Inputs may be any that keep to these rules, and one draw needn't show every extreme that they name: Row t of filled_pillar_positions is a permutation of 0 to 15; an entry c names the column x = c, y = t. `filled_pillar_totals`: some tile has all of its 16 columns occupied.
All inputs are finite; a program needn't handle non-finite values.
Results may differ from the reference program's by a relative error of at most 0.012.
Values may be sent and summed in bfloat16 or wider, within the bound.
No kernel may reach another device: no remote copies, remote signals or barrier semaphores. Data moves between devices by JAX's collectives and lax.ppermute only.
A program may use at most 64 MiB of HBM per device.

```python
import math
import jax
import jax.numpy as jnp
from jax import lax

FEATURE_WIDTH = 512
HEADS = 8
HD = 64
HEIGHT_SITES = 16
ROWS_Y = 1
WIDTH_SITES = 16
DEPTH_SITES = 16
COLS = 16
N_XY = 16


def draw_hidden_features(key, part):
    key = jax.random.fold_in(key, 101)
    entries = jax.random.normal(key, (WIDTH_SITES, HEIGHT_SITES, DEPTH_SITES, FEATURE_WIDTH), jnp.float32)
    return jnp.clip(entries, -6.0, 6.0).astype(jnp.bfloat16)


def draw_attention_input_matrices(key, part):
    key = jax.random.fold_in(key, 202)
    entries = jnp.clip(jax.random.normal(key, (3, FEATURE_WIDTH, 3 * FEATURE_WIDTH), jnp.float32), -6.0, 6.0) * FEATURE_WIDTH ** (-0.5)
    return entries.astype(jnp.bfloat16)


def draw_score_scaling(key, part):
    key = jax.random.fold_in(key, 303)
    lowest, highest = (0.5, 2.0)
    fraction = jax.random.uniform(key, (3, HEADS), jnp.float32)
    return jnp.exp(math.log(lowest) + fraction * (math.log(highest) - math.log(lowest))).astype(jnp.float32)


def draw_filled_pillar_positions(key, part):
    key = jax.random.fold_in(key, 404)
    tile_keys = jax.random.split(key, N_XY)
    return jax.vmap(lambda tile_key: jax.random.permutation(tile_key, COLS))(tile_keys).astype(jnp.int32)


def draw_filled_pillar_totals(key, part):
    key = jax.random.fold_in(key, 505)
    level_key, full_key = jax.random.split(key)
    levels = jax.random.randint(level_key, (N_XY,), 0, 8, dtype=jnp.int32)
    chosen = jax.random.randint(full_key, (), 0, N_XY, dtype=jnp.int32)
    levels = jnp.where(jnp.arange(N_XY, dtype=jnp.int32) == chosen, 7, levels)
    floor_count = COLS // 4
    return (floor_count + (COLS - floor_count) * levels * levels * levels // 343).astype(jnp.int32)


def steps_of(own_key, shape, cuts, least, high):
    factor_of, own = 1.0, jax.random.fold_in(own_key, 6)
    for dim, blocks in cuts:
        draws = jnp.exp(jax.random.uniform(jax.random.fold_in(own, dim), (blocks,), jnp.float32, least / len(cuts), high / len(cuts)))
        factor_of = factor_of * jnp.repeat(draws, shape[dim] // blocks).reshape([-1 if axis == dim else 1 for axis in range(len(shape))])
    return factor_of


def gaussian(rng, shape, width, reach, cuts=(), kind=jnp.bfloat16):
    result = jax.random.normal(rng, shape, jnp.float32) * width
    if len(cuts) > 0:
        result = steps_of(rng, shape, cuts, -0.22, 0.18) * result
    return jnp.clip(result, min=-reach, max=reach).astype(kind)


def setup_inputs(seed: int = 0) -> dict:
    arg_keys = jax.random.split(jax.random.key(seed), 8)
    return {
        "hidden_features": draw_hidden_features(jax.random.fold_in(arg_keys[7], 71), 0),
        "scaling_factors_prenormal": jnp.clip(1.0 + 0.18 * jax.random.normal(arg_keys[1], (FEATURE_WIDTH,), jnp.float32), 0.1, 1.9),
        "attention_input_matrices": draw_attention_input_matrices(jax.random.fold_in(arg_keys[7], 71), 0),
        "final_projection_matrices": gaussian(arg_keys[3], (3, FEATURE_WIDTH, FEATURE_WIDTH), FEATURE_WIDTH ** -0.5, 0.25, ((1, 16),)),
        "score_scaling": draw_score_scaling(jax.random.fold_in(arg_keys[7], 71), 0),
        "filled_pillar_positions": draw_filled_pillar_positions(jax.random.fold_in(arg_keys[7], 71), 0),
        "filled_pillar_totals": draw_filled_pillar_totals(jax.random.fold_in(arg_keys[7], 71), 0),
    }


EPSILON = 1e-06

def rms_scale(vector_rows):
    return vector_rows * lax.rsqrt(lax.optimization_barrier(jnp.mean(vector_rows * vector_rows, axis=-1, keepdims=True)) + EPSILON)

def denoise_single_tile_stack(fiber_length, w_project, w_back, temper_row):
    blocks, positions, channels = fiber_length.shape
    projected = jnp.dot(fiber_length.reshape(blocks * positions, channels), w_project, preferred_element_type=jnp.float32)
    projected = projected.reshape(blocks, positions, 3, HEADS, HD)
    queries = rms_scale(projected[:, :, 0]).astype(jnp.bfloat16)
    key_rows = rms_scale(projected[:, :, 1]).astype(jnp.bfloat16)
    values = projected[:, :, 2].astype(jnp.bfloat16)
    scores = jnp.einsum('bnhd,bmhd->bhnm', queries.astype(jnp.float32), key_rows.astype(jnp.float32))
    scores = scores * (temper_row / math.sqrt(HD))[None, :, None, None]
    weights = jax.nn.softmax(scores, axis=-1).astype(jnp.bfloat16)
    mixture = jnp.einsum('bhnm,bmhd->bnhd', weights.astype(jnp.float32), values.astype(jnp.float32)).astype(jnp.bfloat16)
    tile_stack_answer = jnp.dot(mixture.reshape(blocks * positions, channels), w_back, preferred_element_type=jnp.float32)
    return tile_stack_answer.astype(jnp.bfloat16).reshape(blocks, positions, channels)

def fiber_entries(fiber_length, direction_choice, entries_in_tile_stack, attention_input_matrices, final_projection_matrices, score_scaling):
    count_lines, positions, channels = fiber_length.shape
    gathered_fibers = fiber_length.reshape(count_lines // entries_in_tile_stack, entries_in_tile_stack, positions, channels)
    tile_stack_answer = lax.map(lambda fibers_in_tile_stack: denoise_single_tile_stack(fibers_in_tile_stack, attention_input_matrices[direction_choice], final_projection_matrices[direction_choice], score_scaling[direction_choice]), gathered_fibers)
    return tile_stack_answer.reshape(count_lines, positions, channels)

def tile_occupied(pair_rows):
    order_list, live_count = pair_rows
    spots = jnp.arange(COLS, dtype=jnp.int32)
    matches = order_list[:, None] == spots[None, :]
    live = spots < live_count
    return jnp.any(jnp.logical_and(matches, live[:, None]), axis=0)

def reference(hidden_features, scaling_factors_prenormal, attention_input_matrices, final_projection_matrices, score_scaling, filled_pillar_positions, filled_pillar_totals):
    normed = (rms_scale(hidden_features.astype(jnp.float32)) * scaling_factors_prenormal).astype(jnp.bfloat16)
    mixing_first_direction = jnp.transpose(normed, (1, 2, 0, 3)).reshape(HEIGHT_SITES * DEPTH_SITES, WIDTH_SITES, FEATURE_WIDTH)
    first_direction_answer = fiber_entries(mixing_first_direction, 0, HEIGHT_SITES, attention_input_matrices, final_projection_matrices, score_scaling)
    first_direction_answer = jnp.transpose(first_direction_answer.reshape(HEIGHT_SITES, DEPTH_SITES, WIDTH_SITES, FEATURE_WIDTH), (2, 0, 1, 3))
    mixing_second_direction = normed.reshape(WIDTH_SITES * HEIGHT_SITES, DEPTH_SITES, FEATURE_WIDTH)
    second_direction_answer = fiber_entries(mixing_second_direction, 1, HEIGHT_SITES, attention_input_matrices, final_projection_matrices, score_scaling).reshape(WIDTH_SITES, HEIGHT_SITES, DEPTH_SITES, FEATURE_WIDTH)
    mixing_vertical_direction = jnp.transpose(normed, (0, 2, 1, 3)).reshape(WIDTH_SITES * DEPTH_SITES, HEIGHT_SITES, FEATURE_WIDTH)
    vertical_answer = fiber_entries(mixing_vertical_direction, 2, WIDTH_SITES, attention_input_matrices, final_projection_matrices, score_scaling)
    vertical_answer = jnp.transpose(vertical_answer.reshape(WIDTH_SITES, DEPTH_SITES, HEIGHT_SITES, FEATURE_WIDTH), (0, 2, 1, 3))
    occupied = lax.map(tile_occupied, (filled_pillar_positions, filled_pillar_totals))
    occupied = jnp.transpose(occupied.reshape(N_XY, WIDTH_SITES, ROWS_Y), (1, 0, 2)).reshape(WIDTH_SITES, DEPTH_SITES)
    occupied = occupied.astype(jnp.float32)[:, None, :, None]
    summed = hidden_features.astype(jnp.float32) + first_direction_answer.astype(jnp.float32) + second_direction_answer.astype(jnp.float32)
    summed = summed + vertical_answer.astype(jnp.float32) * occupied
    return summed.astype(jnp.bfloat16)
```

```python
import functools
import math

import jax
import jax.numpy as jnp
from jax import lax
from jax.experimental import pallas as pl
from jax.experimental.pallas import tpu as pltpu
from jax.sharding import PartitionSpec as P

EPSILON = 1e-06


def rms_scale(vector_rows):
    return vector_rows * lax.rsqrt(
        jnp.mean(vector_rows * vector_rows, axis=-1, keepdims=True) + EPSILON
    )


def project_qkv(tokens_in, w_project, attention_parts_number):
    projected = jnp.dot(tokens_in, w_project, preferred_element_type=jnp.float32)
    outer_shape = projected.shape[:-1]
    channels = w_project.shape[0]
    split_rows = projected.reshape(
        outer_shape + (3, attention_parts_number, channels // attention_parts_number)
    )
    queries = (
        rms_scale(split_rows[..., 0, :, :]).reshape(outer_shape + (channels,)).astype(jnp.bfloat16)
    )
    key_rows = (
        rms_scale(split_rows[..., 1, :, :]).reshape(outer_shape + (channels,)).astype(jnp.bfloat16)
    )
    values = split_rows[..., 2, :, :].reshape(outer_shape + (channels,)).astype(jnp.bfloat16)
    return (queries, key_rows, values)


def softmax_over_fibers(queries, key_rows, values, temper_row):
    attention_parts_number = temper_row.shape[0]
    outer_size, query_len, inner_size, channels = queries.shape
    key_len = key_rows.shape[1]
    head_dim = channels // attention_parts_number
    query_heads = queries.reshape(
        outer_size, query_len, inner_size, attention_parts_number, head_dim
    )
    key_heads = key_rows.reshape(outer_size, key_len, inner_size, attention_parts_number, head_dim)
    value_heads = values.reshape(outer_size, key_len, inner_size, attention_parts_number, head_dim)
    scores = jnp.einsum(
        "anbhd,ambhd->abhnm", query_heads, key_heads, preferred_element_type=jnp.float32
    )
    scores = scores * (temper_row / math.sqrt(head_dim))[None, None, :, None, None]
    weights = jax.nn.softmax(scores, axis=-1).astype(jnp.bfloat16)
    mixture = jnp.einsum(
        "abhnm,ambhd->anbhd", weights, value_heads, preferred_element_type=jnp.float32
    )
    return mixture.astype(jnp.bfloat16).reshape(outer_size, query_len, inner_size, channels)


def out_project(mixture, w_back):
    return jnp.dot(mixture, w_back, preferred_element_type=jnp.float32).astype(jnp.bfloat16)


def generic_shards(
    hidden_features,
    scaling_factors_prenormal,
    attention_input_matrices,
    final_projection_matrices,
    score_scaling,
    filled_pillar_positions,
    filled_pillar_totals,
):
    full_qkv, full_out = (
        lax.all_gather(attention_input_matrices, "xy", axis=1, tiled=True),
        lax.all_gather(final_projection_matrices, "xy", axis=1, tiled=True),
    )
    attention_parts_number = score_scaling.shape[1]
    x_local, z_cells, y_rows, channels = hidden_features.shape
    normed = (rms_scale(hidden_features.astype(jnp.float32)) * scaling_factors_prenormal).astype(
        jnp.bfloat16
    )
    y_lines = normed.reshape(x_local * z_cells, y_rows, channels)
    local_query, local_keys, local_values = project_qkv(
        y_lines, full_qkv[1], attention_parts_number
    )
    query_along_y, keys_along_y, values_along_y = (
        lax.all_to_all(local_query, "xy", split_axis=0, concat_axis=1, tiled=True),
        lax.all_to_all(local_keys, "xy", split_axis=0, concat_axis=1, tiled=True),
        lax.all_to_all(local_values, "xy", split_axis=0, concat_axis=1, tiled=True),
    )
    y_mix = softmax_over_fibers(
        query_along_y[:, :, None, :],
        keys_along_y[:, :, None, :],
        values_along_y[:, :, None, :],
        score_scaling[1],
    )[:, :, 0, :]
    second_direction_answer = lax.all_to_all(
        out_project(y_mix, full_out[1]), "xy", split_axis=1, concat_axis=0, tiled=True
    ).reshape(hidden_features.shape)
    pieces = project_qkv(
        lax.all_to_all(normed, "gz", split_axis=1, concat_axis=0, tiled=True),
        full_qkv[0],
        attention_parts_number,
    )
    full_len, slab_part, items, _ = pieces[0].shape
    shaped = (1, full_len, slab_part * items, channels)
    x_mix = softmax_over_fibers(
        pieces[0].reshape(shaped),
        pieces[1].reshape(shaped),
        pieces[2].reshape(shaped),
        score_scaling[0],
    )
    result_rows = out_project(x_mix, full_out[0]).reshape(full_len, slab_part, items, channels)
    first_direction_answer = lax.all_to_all(
        result_rows, "gz", split_axis=0, concat_axis=1, tiled=True
    )
    cols_here = x_local * y_rows
    total_cols = filled_pillar_positions.shape[1]
    my_cols = lax.axis_index("gz") * cols_here + jnp.arange(cols_here, dtype=jnp.int32)
    live_rank = jnp.arange(total_cols, dtype=jnp.int32) < filled_pillar_totals[0]
    matches = filled_pillar_positions[0][None, :] == my_cols[:, None]
    live = jnp.any(jnp.logical_and(matches, live_rank[None, :]), axis=1)
    vertical_asking_terms, vertical_matching_terms, vertical_content_terms = project_qkv(
        normed, full_qkv[2], attention_parts_number
    )
    vertical_blended = softmax_over_fibers(
        vertical_asking_terms, vertical_matching_terms, vertical_content_terms, score_scaling[2]
    )
    z_full = out_project(vertical_blended, full_out[2])
    live_grid = live.reshape(x_local, 1, y_rows, 1)
    vertical_answer = jnp.where(live_grid, z_full, jnp.zeros_like(z_full))
    summed = (
        hidden_features.astype(jnp.float32)
        + first_direction_answer.astype(jnp.float32)
        + second_direction_answer.astype(jnp.float32)
    )
    summed = summed + vertical_answer.astype(jnp.float32)
    return summed.astype(jnp.bfloat16)


LANES = 128
CORES = 2
MASKED = -1e30
BRANCH_CHUNKS = ((1,), (0, 2))


def xy_swap(array, bit, count):
    return lax.ppermute(array, "xy", [(i, i ^ bit) for i in range(count)])


def gz_swap(array):
    return lax.ppermute(array, "gz", [(0, 1), (1, 0)])


def normed_rows(rows, gain):
    wide = rows.astype(jnp.float32)
    return (rms_scale(wide) * gain).astype(jnp.bfloat16)


def my_group():
    core = lax.rem(lax.axis_index("xy"), CORES)
    return CORES * lax.axis_index("gz") + core


def slice_weights_kernel(w_ref, *out_refs):
    channels = w_ref.shape[2] // 3
    core = lax.rem(lax.axis_index("xy"), CORES)
    base = CORES * lax.axis_index("gz")
    for chunk, branches in enumerate(BRANCH_CHUNKS):
        for side, group in enumerate((base + core, base + 1 - core)):
            out_ref = out_refs[2 * chunk + side]
            for n, branch in enumerate(branches):
                for part in range(3):
                    start = pl.multiple_of(part * channels + group * LANES, LANES)
                    out_ref[3 * n + part] = w_ref[branch, :, pl.ds(start, LANES)]


def slice_weights(w_local):
    rows = w_local.shape[1]
    outs = []
    for branches in BRANCH_CHUNKS:
        outs += [jax.ShapeDtypeStruct((3 * len(branches), rows, LANES), w_local.dtype)] * 2
    return pl.pallas_call(slice_weights_kernel, out_shape=outs, name="slice_weights")(w_local)


def place_weights(piece_refs, w_ref, branch_count):
    me = lax.axis_index("xy")
    rows = piece_refs[0].shape[2]
    for offset, piece_ref in enumerate(piece_refs):
        for sub in range(CORES):
            source = lax.bitwise_xor(me, CORES * offset + sub)
            at = pl.ds(pl.multiple_of(source * rows, rows), rows)
            for n in range(branch_count):
                for part in range(3):
                    w_ref[n, at, part * LANES : (part + 1) * LANES] = piece_ref[sub, 3 * n + part]


def attend(tokens, w, scales, same_line, head_dim):
    lane = lax.broadcasted_iota(jnp.int32, (1, LANES), 1)
    first = lane < head_dim
    head_a = lax.broadcasted_iota(jnp.int32, (LANES, LANES), 0) // head_dim
    head_b = lax.broadcasted_iota(jnp.int32, (LANES, LANES), 1) // head_dim
    same_head = (head_a == head_b).astype(jnp.float32).astype(jnp.bfloat16)

    def head_norm(part):
        squares = part * part
        high = squares.astype(jnp.bfloat16)
        low = (squares - high.astype(jnp.float32)).astype(jnp.bfloat16)
        total = jnp.dot(high, same_head, preferred_element_type=jnp.float32) + jnp.dot(
            low, same_head, preferred_element_type=jnp.float32
        )
        return part * lax.rsqrt(total * (1.0 / head_dim) + EPSILON)

    size = same_line.shape[0]
    mixtures = []
    for start in range(0, tokens.shape[0], size):
        projected = jnp.dot(tokens[start : start + size], w, preferred_element_type=jnp.float32)
        queries = head_norm(projected[:, :LANES])
        keys = head_norm(projected[:, LANES : 2 * LANES]).astype(jnp.bfloat16)
        values = projected[:, 2 * LANES :]
        parts = []
        for head in range(2):
            mine = first if head == 0 else jnp.logical_not(first)
            query = jnp.where(mine, queries, 0.0).astype(jnp.bfloat16)
            value = jnp.where(mine, values, 1.0).astype(jnp.bfloat16)
            scores = lax.dot_general(
                query, keys, (((1,), (1,)), ((), ())), preferred_element_type=jnp.float32
            )
            scores = jnp.where(same_line, scores * scales[head], MASKED)
            weights = jnp.exp(scores - jnp.max(scores, axis=1, keepdims=True))
            parts.append(
                jnp.dot(weights.astype(jnp.bfloat16), value, preferred_element_type=jnp.float32)
            )
        mixed = jnp.where(first, parts[0], parts[1])
        total = pltpu.roll(jnp.where(first, parts[1], parts[0]), LANES - head_dim, 1)
        mixtures.append((mixed / total).astype(jnp.bfloat16))
    return mixtures


def line_masks(size, inner):
    a = lax.broadcasted_iota(jnp.int32, (size, size), 0)
    b = lax.broadcasted_iota(jnp.int32, (size, size), 1)
    return lax.rem(a, inner) == lax.rem(b, inner), lax.div(a, inner) == lax.div(b, inner)


def head_scales(scale_ref, branch, head_dim):
    group = my_group()
    return [scale_ref[branch, 2 * group + h] * (1.0 / math.sqrt(head_dim)) for h in range(2)]


def y_kernel(head_dim, scale_ref, t0, t1, t2, t3, gain_ref, *refs):
    piece_refs, out_ref, w_ref = refs[:-2], refs[-2], refs[-1]
    place_weights(piece_refs, w_ref, 1)
    chips, cells, channels = t0.shape
    gain = gain_ref[...]
    tokens = jnp.concatenate(
        [normed_rows(t[...].reshape(chips * cells, channels), gain) for t in (t0, t1, t2, t3)], 0
    )
    same_inner, _ = line_masks(CORES * chips * cells, cells)
    mixtures = attend(tokens, w_ref[0], head_scales(scale_ref, 1, head_dim), same_inner, head_dim)
    for half, mixture in enumerate(mixtures):
        split = mixture.reshape(CORES, chips, cells, LANES)
        for core in range(CORES):
            out_ref[:, core, half] = split[core]


def place_out(keep_ref, came_ref, branch, w_ref):
    me = lax.rem(lax.axis_index("xy"), 2 * CORES)
    rows = keep_ref.shape[2]
    for ref, flip in ((keep_ref, 0), (came_ref, 1)):
        for side in range(2):
            source = lax.bitwise_xor(me, 2 * side + flip)
            w_ref[pl.ds(pl.multiple_of(source * rows, rows), rows), :] = ref[side, branch]


def occupied_rows(pos_ref, gz_index, cells, tokens):
    columns = pos_ref.shape[1] - 1
    bits = jnp.int32(0)
    for n in range(columns):
        bit = lax.shift_left(jnp.int32(1), pos_ref[0, n])
        bits = bits | jnp.where(n < pos_ref[0, columns], bit, 0)
    x_local = tokens // cells
    x = lax.broadcasted_iota(jnp.int32, (tokens, LANES), 0) // cells + gz_index * x_local
    return lax.bitwise_and(lax.shift_right_logical(jnp.full_like(x, bits), x), 1) == 1


def xz_kernel(head_dim, cells, scale_ref, pos_ref, other_ref, n0, n1, m0, m1, gain_ref, keep_ref,
              came_ref, *refs):
    piece_refs, out_ref, w_ref, back_ref = refs[:-3], refs[-3], refs[-2], refs[-1]
    place_weights(piece_refs, w_ref, 2)
    gain = gain_ref[...]
    tokens = jnp.concatenate([normed_rows(t[...], gain) for t in (n0, n1, m0, m1)], 0)
    size = n0.shape[0] * 2
    same_inner, same_outer = line_masks(size, cells)
    place_out(keep_ref, came_ref, 0, back_ref)
    mixtures = attend(tokens, w_ref[0], head_scales(scale_ref, 0, head_dim), same_inner, head_dim)
    for n, mixture in enumerate(mixtures):
        out_ref[n * size : (n + 1) * size] = jnp.dot(
            mixture, back_ref[...], preferred_element_type=jnp.float32
        )
    place_out(keep_ref, came_ref, 2, back_ref)
    mixtures = attend(tokens, w_ref[1], head_scales(scale_ref, 2, head_dim), same_outer, head_dim)
    half = lax.axis_index("gz")
    for n, (mixture, ref) in enumerate(zip(mixtures, (pos_ref, other_ref))):
        live = jnp.concatenate(
            [occupied_rows(ref, half, cells, size // 2), occupied_rows(ref, 1 - half, cells, size // 2)], 0
        )
        mixture = jnp.where(live, mixture.astype(jnp.float32), 0.0).astype(jnp.bfloat16)
        out_ref[n * size : (n + 1) * size] += jnp.dot(
            mixture, back_ref[...], preferred_element_type=jnp.float32
        )


def out_kernel(mix_ref, keep_ref, came_ref, part_ref, own_ref, x_ref, c_ref, xc_ref, back_ref):
    place_out(keep_ref, came_ref, 1, back_ref)
    rows = own_ref.shape[0]
    for core in range(CORES):
        for half in range(2):
            mixture = mix_ref[:, core, half].reshape(rows, LANES)
            n = core * 2 + half
            total = part_ref[n * rows : (n + 1) * rows] + jnp.dot(
                mixture, back_ref[...], preferred_element_type=jnp.float32
            )
            ref = (own_ref, x_ref, c_ref, xc_ref)[n]
            ref[...] = total.astype(ref.dtype)


def vmem_call(kernel, scalars, arrays, out_shape, scratch, name, flops):
    smem = pl.BlockSpec(memory_space=pltpu.SMEM)
    vmem = pl.BlockSpec(memory_space=pltpu.VMEM)
    moved = sum(a.size * a.dtype.itemsize for a in arrays)
    return pl.pallas_call(
        kernel,
        out_shape=out_shape,
        in_specs=[smem] * len(scalars) + [vmem] * len(arrays),
        out_specs=jax.tree.map(lambda _: vmem, out_shape),
        scratch_shapes=scratch,
        name=name,
        cost_estimate=pl.CostEstimate(flops=flops, bytes_accessed=moved, transcendentals=0),
    )(*scalars, *arrays)


def gather_tree(piece, bits, count):
    pieces = [piece]
    for bit in bits:
        pieces = pieces + [xy_swap(p, bit, count) for p in pieces]
    return pieces


def grouped_shards(
    n_xy,
    hidden_features,
    scaling_factors_prenormal,
    attention_input_matrices,
    final_projection_matrices,
    score_scaling,
    filled_pillar_positions,
    filled_pillar_totals,
):
    x_local, z_cells, _, channels = hidden_features.shape
    head_dim = channels // score_scaling.shape[1]
    tokens = x_local * z_cells
    chips = n_xy // CORES
    me, half = lax.axis_index("xy"), lax.axis_index("gz")
    same_core = [[k * CORES + c for k in range(chips)] for c in range(CORES)]
    swap = functools.partial(xy_swap, count=n_xy)

    own = hidden_features.reshape(tokens, channels)
    y_own = lax.all_to_all(
        own.reshape(chips, tokens // chips, channels), "xy", 0, 0, axis_index_groups=same_core, tiled=True
    )
    sliced = slice_weights(attention_input_matrices)

    tree_bits = [1 << b for b in reversed(range(1, n_xy.bit_length() - 1))]
    gathered = []
    for chunk in range(len(BRANCH_CHUNKS)):
        piece = jnp.stack([sliced[2 * chunk], swap(sliced[2 * chunk + 1], 1)])
        gathered.append(gather_tree(piece, tree_bits, n_xy))
    order = [0]
    for bit in tree_bits:
        order = order + [o | bit for o in order]
    gathered = [[pieces[order.index(CORES * k)] for k in range(chips)] for pieces in gathered]

    other = gz_swap(own)
    y_other = gz_swap(y_own)
    y_core, y_cross = swap(y_own, 1), swap(y_other, 1)
    own_core, other_core = swap(own, 1), swap(other, 1)

    top, low, side = n_xy // 2, n_xy // 4, n_xy // 8
    pairs = []
    for i in range(n_xy):
        pairs += [(2 * i + h, 2 * (i ^ top) + h) for h in range(2) if i // top == h]
    came = lax.ppermute(final_projection_matrices, ("xy", "gz"), pairs)
    base = jnp.where(me // top == half, final_projection_matrices, came)
    b, e, d, f = base, swap(base, side), None, None
    d = swap(base, low)
    f = swap(d, side)
    is_low = lax.rem(me // low, 2) == lax.rem(me, CORES)
    low_pair, high_pair = jnp.stack([b, e]), jnp.stack([d, f])
    keep = jnp.where(is_low, low_pair, high_pair)
    back = swap(jnp.where(is_low, high_pair, low_pair), 1)

    columns = jnp.concatenate([filled_pillar_positions, filled_pillar_totals[:, None]], 1)
    other_columns = swap(columns, 1)
    gain = scaling_factors_prenormal[None, :]

    per_branch = 2 * 4 * tokens * channels * 3 * LANES
    y_mix = vmem_call(
        functools.partial(y_kernel, head_dim),
        [score_scaling],
        [y_own, y_core, y_other, y_cross, gain] + gathered[0],
        jax.ShapeDtypeStruct((chips, CORES, 2, z_cells, LANES), jnp.bfloat16),
        [pltpu.VMEM((1, channels, 3 * LANES), jnp.bfloat16)],
        "y_lines",
        per_branch,
    )
    y_mix = lax.all_to_all(y_mix, "xy", 0, 0, axis_index_groups=same_core, tiled=True)
    part = vmem_call(
        functools.partial(xz_kernel, head_dim, z_cells),
        [score_scaling, columns, other_columns],
        [own, other, own_core, other_core, gain, keep, back] + gathered[1],
        jax.ShapeDtypeStruct((4 * tokens, channels), jnp.float32),
        [
            pltpu.VMEM((2, channels, 3 * LANES), jnp.bfloat16),
            pltpu.VMEM((LANES, channels), jnp.bfloat16),
        ],
        "xz_lines",
        2 * per_branch,
    )
    send = jax.ShapeDtypeStruct((tokens, channels), jnp.bfloat16)
    mine, to_gz, to_core, to_both = vmem_call(
        out_kernel,
        [],
        [y_mix, keep, back, part],
        [jax.ShapeDtypeStruct((tokens, channels), jnp.float32), send, send, send],
        [pltpu.VMEM((LANES, channels), jnp.bfloat16)],
        "y_out",
        per_branch // 3,
    )
    both = [(2 * i + h, 2 * (i ^ 1) + 1 - h) for i in range(n_xy) for h in range(2)]
    terms = [gz_swap(to_gz), swap(to_core, 1), lax.ppermute(to_both, ("xy", "gz"), both)]
    total = own.astype(jnp.float32) + mine
    for term in terms:
        total = total + term.astype(jnp.float32)
    return total.astype(jnp.bfloat16).reshape(hidden_features.shape)


def can_group(mesh, hidden, w_back, scales, positions):
    n_xy, n_gz = mesh.shape["xy"], mesh.shape["gz"]
    x_local, z_cells, y_rows, channels = hidden
    heads = scales[1]
    groups = CORES * n_gz
    return (
        n_gz == 2
        and n_xy == 4 * groups
        and y_rows == 1
        and x_local == n_xy // CORES
        and z_cells % 16 == 0
        and heads == 2 * groups
        and channels == groups * LANES
        and w_back[1] * n_xy == channels
        and positions[1] == n_gz * x_local
        and positions[1] <= 31
    )


def solution(mesh):
    in_specs = (
        P("gz", None, "xy", None),
        P(),
        P(None, "xy", None),
        P(None, "xy", None),
        P(),
        P("xy", None),
        P("xy"),
    )
    out_specs = P("gz", None, "xy", None)

    def shards(*args):
        shapes = [a.shape for a in args]
        if can_group(mesh, shapes[0], shapes[3], shapes[4], shapes[5]):
            return grouped_shards(mesh.shape["xy"], *args)
        return generic_shards(*args)

    return jax.shard_map(shards, mesh=mesh, in_specs=in_specs, out_specs=out_specs, check_vma=False)
```
